256 devices in a mesh: grp: 4 (over z_lo, core), row: 4 (over z_hi), col: 16 (over x, y).
Axes of the slice: x: 4, y: 4, z: 8 (z_hi: 4, z_lo: 2; z = z_hi * 2 + z_lo), core: 2. Of those that a mesh axis runs over, the one named last changes fastest.
Arguments:
- pair_rep: bfloat16 [512, 512, 128], P('row', ('grp', 'col')), may hold values from -20 to 20
- residue_index: int32 [512], replicated, may hold values from 0 to 63
- chain_index: int32 [512], replicated, may hold values from 0 to 3, never falling along the last dimension, each value on 1 to 256 neighbouring positions
- token_mask: int32 [512], replicated, may hold values 0 or 1
- relpos_table: bfloat16 [66, 128], replicated, may hold values from -5 to 5
- proj_in: bfloat16 [128, 640], replicated, may hold values from -0.5 to 0.5
- out_proj: bfloat16 [128, 128], replicated, may hold values from -0.5 to 0.5
- bias_weight: float32 [128, 16], replicated, may hold values from -2 to 2
- single_rep: bfloat16 [48, 512, 768], P('col', 'row'), may hold values from -6 to 6
- w_qkvg: bfloat16 [4, 768, 768], P(None, None, 'grp'), may hold values from -0.21875 to 0.21875
- w_out: bfloat16 [768, 768], P('grp'), may hold values from -0.21875 to 0.21875
- cotangent: bfloat16 [48, 512, 768], P('col', 'row'), may hold values from -6 to 6
Outputs:
- pair_out: bfloat16 [512, 512, 128], P('row', ('grp', 'col'))
- single_out: bfloat16 [48, 512, 768], P('col', 'row')
- bias_grad: float32 [16, 512, 512], P('grp', 'row', 'col')
The draws below stay inside these ranges and needn't reach their ends.
All inputs are finite; a program needn't handle non-finite values.
Results may differ from the reference program's by a relative error of at most 0.014.
Values may be sent and summed in bfloat16 or wider, within the bound.
No kernel may reach another device: no remote copies, remote signals or barrier semaphores. Data moves between devices by JAX's collectives and lax.ppermute only.
A program may use at most 64 MiB of HBM per device.

```python
import math
import jax
import jax.numpy as jnp
import numpy as np
from jax import lax

C = 128
H = 16
E = 48
D = 768
TOK_ROW = 128
BINS = 66
N = 512
S = 48
HE = 768
N_ROW = 4


def draw_pair_rep(key, part):
    values = jnp.clip(jax.random.normal(key, (N, N, C), jnp.float32), -6.0, 6.0)
    return values.astype(jnp.bfloat16)


def draw_bias_weight(key, part):
    spread = 2.0 / math.sqrt(C)
    values = jnp.clip(jax.random.normal(key, (C, H), jnp.float32) * spread, -0.9, 0.9)
    return values


def with_ends(entries, stream_key, least, high):
    longest = entries.shape.index(max(entries.shape))
    spots = []
    for shift in (0, 1):
        where = [jax.random.randint(jax.random.fold_in(stream_key, axis), (), 0, length) for axis, length in enumerate(entries.shape)]
        where[longest] = (where[longest] + shift) % entries.shape[longest]
        spots.append(tuple(where))
    return entries.at[spots[0]].set(least).at[spots[1]].set(high)


def steps_of(key, shape, cuts, least, largest):
    factor_of = 1.0
    for position, parts in cuts:
        draws = jax.random.uniform(jax.random.fold_in(jax.random.fold_in(key, 6), position), (parts,), jnp.float32, least / len(cuts), largest / len(cuts))
        factor_of = factor_of * jnp.repeat(jnp.exp(draws), shape[position] // parts).reshape((-1,) + (1,) * (len(shape) - 1 - position))
    return factor_of


def split_up(amount, total, reach, lean):
    weights = [(1 << 20) // math.isqrt(standing ** lean) + 1 for standing in range(2, amount + 1)]
    rest, counts = total - reach - (amount - 1), [1] * (amount - 1)
    while rest > 0:
        candidates = [i for i in range(amount - 1) if counts[i] < reach]
        pool, budget = sum([weights[i] for i in candidates]), rest
        for i in candidates:
            addition = min(reach - counts[i], max(1, budget * weights[i] // pool), rest)
            counts[i] = counts[i] + addition
            rest = rest - addition
    return np.array([reach] + counts)


def ragged_sizes(own_key, amount, total, limit, lean):
    if amount == 2:
        one = jax.random.randint(own_key, (), max(1, total - limit), min(limit, total - 1) + 1)
        return jnp.stack([one, total - one])
    tallies = jnp.asarray(split_up(amount, total, limit, lean), jnp.int32)
    pairs = (amount - 1) // 2
    giver, taker = tallies[1:1 + 2 * pairs:2], tallies[2:2 + 2 * pairs:2]
    slack = jnp.minimum(giver - 1, limit - taker)
    shifted = jax.random.randint(jax.random.fold_in(own_key, 1), (pairs,), 0, 1 << 20) % (slack + 1)
    tallies = tallies.at[1:1 + 2 * pairs:2].set(giver - shifted).at[2:2 + 2 * pairs:2].set(taker + shifted)
    return tallies[jax.random.permutation(jax.random.fold_in(own_key, 2), amount)]


def bell_draw(own_key, shape, scale, bound, cuts=(), kind=jnp.bfloat16):
    values = scale * jax.random.normal(own_key, shape, jnp.float32)
    if cuts:
        values = values * steps_of(own_key, shape, cuts, -0.22, 0.18)
    return jnp.clip(values, -bound, bound).astype(kind)


def setup_inputs(seed: int = 0) -> dict:
    key_list = jax.random.split(jax.random.key(seed), 13)
    return {
        "pair_rep": draw_pair_rep(jax.random.fold_in(key_list[12], 71), 0),
        "residue_index": with_ends(jax.random.randint(key_list[1], (N,), 0, 64), jax.random.fold_in(key_list[1], 1), 0, 63).astype(jnp.int32),
        "chain_index": jnp.searchsorted(jnp.cumsum(ragged_sizes(key_list[2], 4, N, N // 2, 1)), jnp.arange(N), side="right").astype(jnp.int32),
        "token_mask": with_ends((jax.random.randint(key_list[3], (N,), 0, 8) < 7).astype(jnp.int32), jax.random.fold_in(key_list[3], 1), 0, 1),
        "relpos_table": bell_draw(key_list[4], (BINS, C), 1.0, 5.0),
        "proj_in": bell_draw(key_list[5], (C, 5 * C), C ** -0.5, 0.5),
        "out_proj": bell_draw(key_list[6], (C, C), C ** -0.5, 0.5),
        "bias_weight": draw_bias_weight(jax.random.fold_in(key_list[12], 71), 0),
        "single_rep": bell_draw(key_list[8], (S, N, D), 1.0, 6.0, ((0, 16), (1, 4))),
        "w_qkvg": bell_draw(key_list[9], (4, D, HE), D ** -0.5, 0.21875, ((2, 4),)),
        "w_out": bell_draw(key_list[10], (HE, D), HE ** -0.5, 0.21875, ((0, 4),)),
        "cotangent": bell_draw(key_list[11], (S, N, D), 1.0, 6.0, ((0, 16), (1, 4))),
    }


def normalize(values, axis_at):
    average = lax.optimization_barrier(jnp.mean(values, axis=axis_at, keepdims=True))
    centred = values - average
    variance = lax.optimization_barrier(jnp.mean(centred * centred, axis=axis_at, keepdims=True))
    return centred * lax.rsqrt(variance + 1e-05)

def widen(values):
    return lax.optimization_barrier(values).astype(jnp.float32)

def reference(pair_rep, residue_index, chain_index, token_mask, relpos_table, proj_in, out_proj, bias_weight, single_rep, w_qkvg, w_out, cotangent):
    table_f = relpos_table.astype(jnp.float32)
    highest = lax.Precision.HIGHEST

    def front(block_at):
        start_at = (block_at * TOK_ROW).astype(jnp.int32)
        pair_rows = lax.dynamic_slice_in_dim(pair_rep, start_at, TOK_ROW, 0).astype(jnp.float32)
        res_rows = lax.dynamic_slice_in_dim(residue_index, start_at, TOK_ROW, 0)
        chain_rows = lax.dynamic_slice_in_dim(chain_index, start_at, TOK_ROW, 0)
        mask_rows = lax.dynamic_slice_in_dim(token_mask, start_at, TOK_ROW, 0)
        offsets = jnp.clip(res_rows[:, None] - residue_index[None, :], -32, 32) + 32
        bin_ids = jnp.where(chain_rows[:, None] == chain_index[None, :], offsets, 65).astype(jnp.int32)
        pair_in = pair_rows + table_f[bin_ids]
        normed = normalize(pair_in, 2).astype(jnp.bfloat16)
        projected = jnp.dot(normed.reshape(-1, C), proj_in, preferred_element_type=jnp.float32).reshape(TOK_ROW, N, 5 * C)
        pair_mask = (mask_rows[:, None] * token_mask[None, :]).astype(jnp.float32)[:, :, None]
        left_in = (jax.nn.sigmoid(projected[:, :, 2 * C:3 * C]) * projected[:, :, :C] * pair_mask).astype(jnp.bfloat16)
        right_in = (jax.nn.sigmoid(projected[:, :, 3 * C:4 * C]) * projected[:, :, C:2 * C] * pair_mask).astype(jnp.bfloat16)
        gate_out = jax.nn.sigmoid(projected[:, :, 4 * C:])
        return (pair_in, left_in, right_in, gate_out)
    block_ids = jnp.arange(N_ROW, dtype=jnp.int32)
    lefts, rights = lax.map(lambda block_at: front(block_at)[1:3], block_ids)
    left_t = jnp.moveaxis(lefts.reshape(N, N, C), 2, 0)
    right_t = jnp.moveaxis(rights.reshape(N, N, C), 2, 0)

    def channel(operands):
        return jnp.dot(operands[0].T, operands[1], preferred_element_type=jnp.float32).astype(jnp.bfloat16)
    triangle = lax.map(channel, (left_t, right_t))

    def finish(block_at):
        pair_in, unused_left, unused_right, gate_out = front(block_at)
        start_at = (block_at * TOK_ROW).astype(jnp.int32)
        tri_rows = lax.dynamic_slice_in_dim(triangle, start_at, TOK_ROW, 1).astype(jnp.float32)
        out_normed = normalize(tri_rows, 0).astype(jnp.bfloat16)
        update = jnp.einsum('cij,cd->ijd', widen(out_normed), out_proj.astype(jnp.float32), precision=highest)
        pair_new = pair_in + gate_out * update
        bias_rows = jnp.einsum('ijc,ch->hij', normalize(pair_new, 2), bias_weight, precision=highest)
        return (pair_new.astype(jnp.bfloat16), bias_rows)
    new_rows, bias_rows = lax.map(finish, block_ids)
    pair_out = new_rows.reshape(N, N, C)
    pair_bias = jnp.moveaxis(bias_rows, 0, 1).reshape(H, N, N)
    keep = (token_mask == 1)[None, None, :]
    scale_qk = 1.0 / math.sqrt(E)

    def sample(carry, items):
        tokens_x, grad_y = items
        normed_x = normalize(tokens_x.astype(jnp.float32), 1).astype(jnp.bfloat16)
        queries = jnp.dot(normed_x, w_qkvg[0], preferred_element_type=jnp.float32).astype(jnp.bfloat16).reshape(N, H, E)
        key_rows = jnp.dot(normed_x, w_qkvg[1], preferred_element_type=jnp.float32).astype(jnp.bfloat16).reshape(N, H, E)
        value_rows = jnp.dot(normed_x, w_qkvg[2], preferred_element_type=jnp.float32).astype(jnp.bfloat16).reshape(N, H, E)
        gate_in = jax.nn.sigmoid(jnp.dot(normed_x, w_qkvg[3], preferred_element_type=jnp.float32))
        scores = jnp.einsum('ihe,jhe->hij', widen(queries), widen(key_rows), precision=highest) * scale_qk + pair_bias
        scores = jnp.where(keep, scores, -1000000000.0)
        top_score = lax.optimization_barrier(jnp.max(scores, axis=-1, keepdims=True))
        weights = jnp.exp(scores - top_score)
        probs = weights / lax.optimization_barrier(jnp.sum(weights, axis=-1, keepdims=True))
        mixed = jnp.einsum('hij,jhe->ihe', widen(probs.astype(jnp.bfloat16)), widen(value_rows), precision=highest).reshape(N, H * E)
        gated = (mixed * gate_in).astype(jnp.bfloat16)
        output = (tokens_x.astype(jnp.float32) + jnp.dot(gated, w_out, preferred_element_type=jnp.float32)).astype(jnp.bfloat16)
        back_rows = jnp.dot(grad_y, w_out.T, preferred_element_type=jnp.float32)
        d_mixed = (back_rows * gate_in).astype(jnp.bfloat16).reshape(N, H, E)
        d_probs = jnp.einsum('ihe,jhe->hij', widen(d_mixed), widen(value_rows), precision=highest)
        inner = lax.optimization_barrier(jnp.sum(probs * d_probs, axis=-1, keepdims=True))
        return (carry + probs * (d_probs - inner), output)
    bias_grad, single_out = lax.scan(sample, jnp.zeros((H, N, N), jnp.float32), (single_rep, cotangent))
    return (pair_out, single_out, bias_grad)
```

```python
import math

import jax
import jax.numpy as jnp
from jax import lax
from jax.experimental import pallas as pl
from jax.experimental.pallas import tpu as pltpu
from jax.sharding import PartitionSpec as P

BF = jnp.bfloat16
F32 = jnp.float32


def normalize(values, axis_at):
    average = jnp.mean(values, axis=axis_at, keepdims=True)
    centred = values - average
    variance = jnp.mean(centred * centred, axis=axis_at, keepdims=True)
    return centred * lax.rsqrt(variance + 1e-05)


def attention_kernel(
    heads,
    head_size,
    row_ref,
    qt_ref,
    dmt_ref,
    gt_ref,
    kv0_ref,
    kv1_ref,
    kv2_ref,
    kv3_ref,
    bias_ref,
    gated_ref,
    grad_ref,
    k_s,
    v_s,
    qbd,
    dbd,
    st,
    dpt,
    pt,
    gacc,
):
    samples, width, rows = qt_ref.shape
    row_count = 4
    keys = rows * row_count
    scale = 1.0 / math.sqrt(head_size)
    row_at = row_ref[0]
    qbd[...] = jnp.zeros_like(qbd)
    dbd[...] = jnp.zeros_like(dbd)
    chunk = 64
    groups = chunk // 8

    def one_sample(s, unused):
        for step, ref in enumerate((kv0_ref, kv1_ref, kv2_ref, kv3_ref)):
            block = lax.rem(row_at + row_count - step, row_count)
            at = pl.multiple_of(block * rows, rows)
            k_s[pl.ds(at, rows), :] = ref[s, :, 0:width]
            v_s[pl.ds(at, rows), :] = ref[s, :, width : 2 * width]
        for h in range(heads):
            e0, i0 = h * head_size, h * rows
            qbd[e0 : e0 + head_size, i0 : i0 + rows] = qt_ref[s, e0 : e0 + head_size, :]
            dbd[e0 : e0 + head_size, i0 : i0 + rows] = dmt_ref[s, e0 : e0 + head_size, :]
        st[...] = jnp.dot(k_s[...], qbd[...], preferred_element_type=F32)
        dpt[...] = jnp.dot(v_s[...], dbd[...], preferred_element_type=F32)
        for h in range(heads):
            e0, i0 = h * head_size, h * rows
            lanes = slice(i0, i0 + rows)
            top = jnp.full((8, rows), -jnp.inf, F32)
            for b in range(keys // chunk):
                part = slice(b * chunk, (b + 1) * chunk)
                bias = bias_ref[b * groups : (b + 1) * groups, h, :, :].reshape(chunk, rows)
                x = st[part, lanes] * scale + bias
                st[part, lanes] = x
                top = jnp.maximum(top, jnp.max(x.reshape(groups, 8, rows), axis=0))
            peak = jnp.max(top, axis=0, keepdims=True)
            total = jnp.zeros((8, rows), F32)
            dots = jnp.zeros((8, rows), F32)
            for b in range(keys // chunk):
                part = slice(b * chunk, (b + 1) * chunk)
                w = jnp.exp(st[part, lanes] - peak)
                st[part, lanes] = w
                total = total + jnp.sum(w.reshape(groups, 8, rows), axis=0)
                dots = dots + jnp.sum((w * dpt[part, lanes]).reshape(groups, 8, rows), axis=0)
            inverse = 1.0 / jnp.sum(total, axis=0, keepdims=True)
            inner = jnp.sum(dots, axis=0, keepdims=True) * inverse
            for b in range(keys // chunk):
                part = slice(b * chunk, (b + 1) * chunk)
                p = st[part, lanes] * inverse
                pt[part, lanes] = p.astype(BF)
                d = p * (dpt[part, lanes] - inner)

                @pl.when(s == 0)
                def _():
                    gacc[h, part, :] = d

                @pl.when(s > 0)
                def _():
                    gacc[h, part, :] = gacc[h, part, :] + d

            mixed = lax.dot_general(
                v_s[...],
                pt[:, lanes],
                (((0,), (0,)), ((), ())),
                preferred_element_type=F32,
            )
            gated_ref[s, e0 : e0 + head_size, :] = (
                mixed[e0 : e0 + head_size, :] * gt_ref[s, e0 : e0 + head_size, :]
            ).astype(BF)
        return unused

    lax.fori_loop(0, samples, one_sample, 0)
    parts, _, width_j, _ = grad_ref.shape
    for h in range(heads):
        for c in range(parts):
            grad_ref[c, h, :, :] = gacc[h, c * width_j : (c + 1) * width_j, :].astype(BF)


def on_device(
    pair_rep,
    residue_index,
    chain_index,
    token_mask,
    relpos_table,
    proj_in,
    out_proj,
    bias_weight,
    single_rep,
    w_qkvg,
    w_out,
    cotangent,
):
    tok_rows, col_width, channels = pair_rep.shape
    col_count = lax.axis_size("col")
    grp_count = lax.axis_size("grp")
    row_count = lax.axis_size("row")
    row_at = lax.axis_index("row")
    grp_at = lax.axis_index("grp")
    col_at = lax.axis_index("col")
    total_tok = residue_index.shape[0]
    samples = single_rep.shape[0]
    head_width = w_out.shape[0]
    all_heads = bias_weight.shape[1]
    heads = all_heads // grp_count
    head_size = head_width // heads
    row_start = row_at * tok_rows
    col_start = (grp_at * col_count + col_at) * col_width
    table = jnp.stack([residue_index, chain_index, token_mask])
    of_rows = lax.dynamic_slice_in_dim(table, row_start, tok_rows, 1)
    of_cols = lax.dynamic_slice_in_dim(table, col_start, col_width, 1)
    mask_rows, mask_cols = of_rows[2], of_cols[2]

    normed_x = normalize(single_rep.astype(F32), 2).astype(BF)
    key_value = jnp.einsum(
        "srd,tde->srte", normed_x, w_qkvg[1:3], preferred_element_type=F32
    )
    keep_rows = (mask_rows == 1)[None, :, None, None]
    is_value = (jnp.arange(2) == 1)[None, None, :, None]
    key_value = jnp.where(keep_rows | is_value, key_value, 0.0).astype(BF)
    key_value = key_value.reshape(samples, tok_rows, 2 * head_width)
    with jax.named_scope("kvshift"):
        moved = [
            lax.ppermute(
                key_value, "row", [(i, (i + step) % row_count) for i in range(row_count)]
            )
            for step in range(1, row_count)
        ]

    pair_tile = pair_rep.transpose(1, 0, 2).astype(F32)
    offsets = jnp.clip(of_rows[0][None, :] - of_cols[0][:, None], -32, 32) + 32
    bin_ids = jnp.where(of_rows[1][None, :] == of_cols[1][:, None], offsets, 65)
    onehot = (
        bin_ids[:, :, None] == jnp.arange(relpos_table.shape[0], dtype=jnp.int32)[None, None, :]
    ).astype(BF)
    pair_in = pair_tile + jnp.einsum(
        "jib,bc->jic", onehot, relpos_table, preferred_element_type=F32
    )
    normed = normalize(pair_in, 2).astype(BF)
    projected = jnp.einsum(
        "jic,ce->eji", normed, proj_in[:, : 4 * channels], preferred_element_type=F32
    )
    pair_mask = (mask_cols[:, None] * mask_rows[None, :]).astype(F32)[None]
    left_in = (
        jax.nn.sigmoid(projected[2 * channels : 3 * channels]) * projected[:channels] * pair_mask
    ).astype(BF)
    right_in = (
        jax.nn.sigmoid(projected[3 * channels :]) * projected[channels : 2 * channels] * pair_mask
    ).astype(BF)
    half = col_width // 2
    everyone = ("row", "col", "grp")
    count = row_count * col_count * grp_count
    send = jnp.stack(
        [
            left_in.reshape(channels, 2, half, tok_rows),
            right_in.reshape(channels, 2, half, tok_rows),
        ],
        axis=2,
    ).reshape(count, 2 * half, tok_rows)
    with jax.named_scope("spread"):
        got = lax.all_to_all(send, everyone, 0, 0, tiled=True)
    got = got.reshape(row_count, col_count, grp_count, 2, half, tok_rows)
    left_own, right_own = got[:, :, :, 0], got[:, :, :, 1]
    with jax.named_scope("coreswap"):
        left_other = lax.ppermute(left_own, "grp", [(i, i ^ 1) for i in range(grp_count)])
    first = (grp_at % 2) == 0
    left_all = jnp.stack(
        [jnp.where(first, left_own, left_other), jnp.where(first, left_other, left_own)], axis=3
    )
    triangle = jnp.einsum(
        "rcghqk,rCGQk->gCGQchq", left_all, right_own, preferred_element_type=F32
    )
    back = triangle.astype(BF).reshape(count, half, tok_rows)
    with jax.named_scope("return"):
        tri_local = lax.all_to_all(back, everyone, 0, 0, tiled=True)
    tri_local = tri_local.reshape(channels, col_width, tok_rows)
    out_normed = normalize(tri_local.astype(F32), 0).astype(BF)
    gate_out = jax.nn.sigmoid(
        jnp.einsum("jic,cd->jid", normed, proj_in[:, 4 * channels :], preferred_element_type=F32)
    )
    update = jnp.einsum("cji,cd->jid", out_normed, out_proj, preferred_element_type=F32)
    pair_new = pair_in + gate_out * update
    pair_out = pair_new.astype(BF).transpose(1, 0, 2)
    bias_local = jnp.einsum(
        "jic,ch->hji", normalize(pair_new, 2), bias_weight, precision=lax.Precision.HIGHEST
    )
    bias_local = jnp.where((mask_cols == 1)[None, :, None], bias_local, -1000000000.0)
    copies = jnp.broadcast_to(
        bias_local.reshape(grp_count, 1, heads, col_width, tok_rows),
        (grp_count, col_count, heads, col_width, tok_rows),
    ).reshape(grp_count * col_count, heads, col_width, tok_rows)
    with jax.named_scope("biasspread"):
        bias_all = lax.all_to_all(copies, ("grp", "col"), 0, 0, tiled=True)

    query_t = jnp.einsum("srd,de->ser", normed_x, w_qkvg[0], preferred_element_type=F32).astype(BF)
    gate_t = jax.nn.sigmoid(
        jnp.einsum("srd,de->ser", normed_x, w_qkvg[3], preferred_element_type=F32)
    )
    back_t = jnp.einsum("srd,ed->ser", cotangent, w_out, preferred_element_type=F32)
    d_mixed_t = (back_t * gate_t).astype(BF)
    with jax.named_scope("wgather"):
        weights = [w_out] + [
            lax.ppermute(w_out, "grp", [(i, i ^ m) for i in range(grp_count)])
            for m in range(1, grp_count)
        ]
    keys = row_count * tok_rows
    vmem = pl.BlockSpec(memory_space=pltpu.VMEM)
    gated_t, grads = pl.pallas_call(
        lambda *refs: attention_kernel(heads, head_size, *refs),
        out_shape=(
            jax.ShapeDtypeStruct((samples, head_width, tok_rows), BF),
            jax.ShapeDtypeStruct((col_count, heads, keys // col_count, tok_rows), BF),
        ),
        in_specs=[pl.BlockSpec(memory_space=pltpu.SMEM)] + [vmem] * 8,
        out_specs=(vmem, vmem),
        scratch_shapes=[
            pltpu.VMEM((keys, head_width), BF),
            pltpu.VMEM((keys, head_width), BF),
            pltpu.VMEM((head_width, heads * tok_rows), BF),
            pltpu.VMEM((head_width, heads * tok_rows), BF),
            pltpu.VMEM((keys, heads * tok_rows), F32),
            pltpu.VMEM((keys, heads * tok_rows), F32),
            pltpu.VMEM((keys, heads * tok_rows), BF),
            pltpu.VMEM((heads, keys, tok_rows), F32),
        ],
        name="attention",
    )(
        row_at.astype(jnp.int32).reshape(1),
        query_t,
        d_mixed_t,
        gate_t,
        key_value,
        *moved,
        bias_all,
    )
    with jax.named_scope("gatedgather"):
        gated_parts = [gated_t] + [
            lax.ppermute(gated_t, "grp", [(i, i ^ m) for i in range(grp_count)])
            for m in range(1, grp_count)
        ]
    with jax.named_scope("gradspread"):
        grad_parts = lax.all_to_all(grads, "col", 0, 0, tiled=True)
    grad_sum = jnp.sum(grad_parts.astype(F32), axis=0)
    bias_grad = grad_sum.transpose(0, 2, 1)
    mixed_out = jnp.einsum(
        "ser,ed->srd",
        jnp.concatenate(gated_parts, axis=1),
        jnp.concatenate(weights, axis=0),
        preferred_element_type=F32,
    )
    single_out = (single_rep.astype(F32) + mixed_out).astype(BF)
    return (pair_out, single_out, bias_grad)


def solution(mesh):
    placed = (
        P("row", ("grp", "col"), None),
        P(),
        P(),
        P(),
        P(),
        P(),
        P(),
        P(),
        P("col", "row", None),
        P(None, None, "grp"),
        P("grp", None),
        P("col", "row", None),
    )
    return jax.shard_map(
        on_device,
        mesh=mesh,
        in_specs=placed,
        out_specs=(P("row", ("grp", "col"), None), P("col", "row", None), P("grp", "row", "col")),
        check_vma=False,
    )
```

```python
import math

import jax
import jax.numpy as jnp
from jax import lax
from jax.experimental import pallas as pl
from jax.experimental.pallas import tpu as pltpu
from jax.sharding import PartitionSpec as P

BF = jnp.bfloat16
F32 = jnp.float32


def normalize(values, axis_at):
    average = jnp.mean(values, axis=axis_at, keepdims=True)
    centred = values - average
    variance = jnp.mean(centred * centred, axis=axis_at, keepdims=True)
    return centred * lax.rsqrt(variance + 1e-05)


def gather_grp(value, axis_at):
    size = lax.axis_size("grp")
    far = lax.ppermute(value, "grp", [(i, i ^ 2) for i in range(size)])
    both = jnp.concatenate([value, far], axis=axis_at)
    near = lax.ppermute(both, "grp", [(i, i ^ 1) for i in range(size)])
    return jnp.concatenate([both, near], axis=axis_at)


def attention_kernel(
    heads,
    head_size,
    row_ref,
    qt_ref,
    dmt_ref,
    gt_ref,
    kv0_ref,
    kv1_ref,
    kv2_ref,
    kv3_ref,
    bias_ref,
    gated_ref,
    grad_ref,
    k_s,
    v_s,
    qbd,
    dbd,
    st,
    dpt,
    pt,
    gacc,
):
    samples, width, rows = qt_ref.shape
    row_count = 4
    keys = rows * row_count
    scale = 1.0 / math.sqrt(head_size)
    row_at = row_ref[0]
    qbd[...] = jnp.zeros_like(qbd)
    dbd[...] = jnp.zeros_like(dbd)
    chunk = 64
    groups = chunk // 8

    def one_sample(s, unused):
        for step, ref in enumerate((kv0_ref, kv1_ref, kv2_ref, kv3_ref)):
            block = lax.rem(row_at + row_count - step, row_count)
            at = pl.multiple_of(block * rows, rows)
            k_s[pl.ds(at, rows), :] = ref[s, :, 0:width]
            v_s[pl.ds(at, rows), :] = ref[s, :, width : 2 * width]
        for h in range(heads):
            e0, i0 = h * head_size, h * rows
            qbd[e0 : e0 + head_size, i0 : i0 + rows] = qt_ref[s, e0 : e0 + head_size, :]
            dbd[e0 : e0 + head_size, i0 : i0 + rows] = dmt_ref[s, e0 : e0 + head_size, :]
        st[...] = jnp.dot(k_s[...], qbd[...], preferred_element_type=F32)
        dpt[...] = jnp.dot(v_s[...], dbd[...], preferred_element_type=F32)
        for h in range(heads):
            e0, i0 = h * head_size, h * rows
            lanes = slice(i0, i0 + rows)
            top = jnp.full((8, rows), -jnp.inf, F32)
            for b in range(keys // chunk):
                part = slice(b * chunk, (b + 1) * chunk)
                bias = bias_ref[b * groups : (b + 1) * groups, h, :, :].reshape(chunk, rows)
                x = st[part, lanes] * scale + bias
                st[part, lanes] = x
                top = jnp.maximum(top, jnp.max(x.reshape(groups, 8, rows), axis=0))
            peak = jnp.max(top, axis=0, keepdims=True)
            total = jnp.zeros((8, rows), F32)
            dots = jnp.zeros((8, rows), F32)
            for b in range(keys // chunk):
                part = slice(b * chunk, (b + 1) * chunk)
                w = jnp.exp(st[part, lanes] - peak)
                st[part, lanes] = w
                total = total + jnp.sum(w.reshape(groups, 8, rows), axis=0)
                dots = dots + jnp.sum((w * dpt[part, lanes]).reshape(groups, 8, rows), axis=0)
            inverse = 1.0 / jnp.sum(total, axis=0, keepdims=True)
            inner = jnp.sum(dots, axis=0, keepdims=True) * inverse
            for b in range(keys // chunk):
                part = slice(b * chunk, (b + 1) * chunk)
                p = st[part, lanes] * inverse
                pt[part, lanes] = p.astype(BF)
                d = p * (dpt[part, lanes] - inner)

                @pl.when(s == 0)
                def _():
                    gacc[h, part, :] = d

                @pl.when(s > 0)
                def _():
                    gacc[h, part, :] = gacc[h, part, :] + d

            mixed = lax.dot_general(
                v_s[...],
                pt[:, lanes],
                (((0,), (0,)), ((), ())),
                preferred_element_type=F32,
            )
            gated_ref[s, e0 : e0 + head_size, :] = (
                mixed[e0 : e0 + head_size, :] * gt_ref[s, e0 : e0 + head_size, :]
            ).astype(BF)
        return unused

    lax.fori_loop(0, samples, one_sample, 0)
    parts, _, width_j, _ = grad_ref.shape
    for h in range(heads):
        for c in range(parts):
            grad_ref[c, h, :, :] = gacc[h, c * width_j : (c + 1) * width_j, :].astype(BF)


def on_device(
    pair_rep,
    residue_index,
    chain_index,
    token_mask,
    relpos_table,
    proj_in,
    out_proj,
    bias_weight,
    single_rep,
    w_qkvg,
    w_out,
    cotangent,
):
    tok_rows, col_width, channels = pair_rep.shape
    col_count = lax.axis_size("col")
    grp_count = lax.axis_size("grp")
    row_count = lax.axis_size("row")
    row_at = lax.axis_index("row")
    grp_at = lax.axis_index("grp")
    col_at = lax.axis_index("col")
    samples = single_rep.shape[0]
    head_width = w_out.shape[0]
    all_heads = bias_weight.shape[1]
    heads = all_heads // grp_count
    head_size = head_width // heads
    row_start = row_at * tok_rows
    col_start = (grp_at * col_count + col_at) * col_width
    table = jnp.stack([residue_index, chain_index, token_mask])
    of_rows = lax.dynamic_slice_in_dim(table, row_start, tok_rows, 1)
    of_cols = lax.dynamic_slice_in_dim(table, col_start, col_width, 1)
    mask_rows, mask_cols = of_rows[2], of_cols[2]

    normed_x = normalize(single_rep.astype(F32), 2).astype(BF)
    key_value = jnp.einsum(
        "srd,tde->srte", normed_x, w_qkvg[1:3], preferred_element_type=F32
    )
    keep_rows = (mask_rows == 1)[None, :, None, None]
    is_value = (jnp.arange(2) == 1)[None, None, :, None]
    key_value = jnp.where(keep_rows | is_value, key_value, 0.0).astype(BF)
    key_value = key_value.reshape(samples, tok_rows, 2 * head_width)
    moved = [
        lax.ppermute(
            key_value, "row", [(i, (i + step) % row_count) for i in range(row_count)]
        )
        for step in range(1, row_count)
    ]

    pair_tile = pair_rep.transpose(1, 0, 2).astype(F32)
    offsets = jnp.clip(of_rows[0][None, :] - of_cols[0][:, None], -32, 32) + 32
    bin_ids = jnp.where(of_rows[1][None, :] == of_cols[1][:, None], offsets, 65)
    onehot = (
        bin_ids[:, :, None] == jnp.arange(relpos_table.shape[0], dtype=jnp.int32)[None, None, :]
    ).astype(BF)
    pair_in = pair_tile + jnp.einsum(
        "jib,bc->jic", onehot, relpos_table, preferred_element_type=F32
    )
    normed = normalize(pair_in, 2).astype(BF)
    projected = jnp.einsum(
        "jic,ce->eji", normed, proj_in[:, : 4 * channels], preferred_element_type=F32
    )
    pair_mask = (mask_cols[:, None] * mask_rows[None, :]).astype(F32)[None]
    left_in = (
        jax.nn.sigmoid(projected[2 * channels : 3 * channels]) * projected[:channels] * pair_mask
    ).astype(BF)
    right_in = (
        jax.nn.sigmoid(projected[3 * channels :]) * projected[channels : 2 * channels] * pair_mask
    ).astype(BF)
    half = col_width // 2
    everyone = ("row", "col", "grp")
    count = row_count * col_count * grp_count
    send = jnp.stack(
        [
            left_in.reshape(channels, 2, half, tok_rows),
            right_in.reshape(channels, 2, half, tok_rows),
        ],
        axis=2,
    ).reshape(count, 2 * half, tok_rows)
    got = lax.all_to_all(send, everyone, 0, 0, tiled=True)
    got = got.reshape(row_count, col_count, grp_count, 2, half, tok_rows)
    left_own, right_own = got[:, :, :, 0], got[:, :, :, 1]
    left_other = lax.ppermute(left_own, "grp", [(i, i ^ 1) for i in range(grp_count)])
    first = (grp_at % 2) == 0
    left_all = (
        jnp.stack(
            [jnp.where(first, left_own, left_other), jnp.where(first, left_other, left_own)],
            axis=3,
        )
        .transpose(0, 2, 1, 3, 4, 5)
        .reshape(row_count, grp_count, tok_rows, tok_rows)
    )
    right_all = right_own.reshape(row_count, count * half // row_count, tok_rows)
    triangle = jnp.einsum("rgik,rjk->gji", left_all, right_all, preferred_element_type=F32)
    back = triangle.astype(BF).reshape(count, half, tok_rows)
    tri_local = lax.all_to_all(back, everyone, 0, 0, tiled=True)
    tri_local = tri_local.reshape(channels, col_width, tok_rows)
    out_normed = normalize(tri_local.astype(F32), 0).astype(BF)
    gate_out = jax.nn.sigmoid(
        jnp.einsum("jic,cd->jid", normed, proj_in[:, 4 * channels :], preferred_element_type=F32)
    )
    update = jnp.einsum("cji,cd->jid", out_normed, out_proj, preferred_element_type=F32)
    pair_new = pair_in + gate_out * update
    pair_out = pair_new.astype(BF).transpose(1, 0, 2)
    bias_local = jnp.einsum(
        "jic,ch->hji", normalize(pair_new, 2), bias_weight, precision=lax.Precision.HIGHEST
    )
    bias_local = jnp.where((mask_cols == 1)[None, :, None], bias_local, -1000000000.0)
    copies = jnp.broadcast_to(
        bias_local.reshape(grp_count, 1, heads, col_width, tok_rows),
        (grp_count, col_count, heads, col_width, tok_rows),
    ).reshape(grp_count * col_count, heads, col_width, tok_rows)
    bias_all = lax.all_to_all(copies, ("grp", "col"), 0, 0, tiled=True)

    query_t = jnp.einsum("srd,de->ser", normed_x, w_qkvg[0], preferred_element_type=F32).astype(BF)
    gate_t = jax.nn.sigmoid(
        jnp.einsum("srd,de->ser", normed_x, w_qkvg[3], preferred_element_type=F32)
    )
    back_t = jnp.einsum("srd,ed->ser", cotangent, w_out, preferred_element_type=F32)
    d_mixed_t = (back_t * gate_t).astype(BF)
    weights = gather_grp(w_out, 0)
    keys = row_count * tok_rows
    vmem = pl.BlockSpec(memory_space=pltpu.VMEM)
    gated_t, grads = pl.pallas_call(
        lambda *refs: attention_kernel(heads, head_size, *refs),
        out_shape=(
            jax.ShapeDtypeStruct((samples, head_width, tok_rows), BF),
            jax.ShapeDtypeStruct((col_count, heads, keys // col_count, tok_rows), BF),
        ),
        in_specs=[pl.BlockSpec(memory_space=pltpu.SMEM)] + [vmem] * 8,
        out_specs=(vmem, vmem),
        scratch_shapes=[
            pltpu.VMEM((keys, head_width), BF),
            pltpu.VMEM((keys, head_width), BF),
            pltpu.VMEM((head_width, heads * tok_rows), BF),
            pltpu.VMEM((head_width, heads * tok_rows), BF),
            pltpu.VMEM((keys, heads * tok_rows), F32),
            pltpu.VMEM((keys, heads * tok_rows), F32),
            pltpu.VMEM((keys, heads * tok_rows), BF),
            pltpu.VMEM((heads, keys, tok_rows), F32),
        ],
        name="attention",
    )(
        row_at.astype(jnp.int32).reshape(1),
        query_t,
        d_mixed_t,
        gate_t,
        key_value,
        *moved,
        bias_all,
    )
    gated_parts = gather_grp(gated_t, 1)
    grad_parts = lax.all_to_all(grads, "col", 0, 0, tiled=True)
    grad_sum = jnp.sum(grad_parts.astype(F32), axis=0)
    bias_grad = grad_sum.transpose(0, 2, 1)
    mixed_out = jnp.einsum(
        "ser,ed->srd",
        gated_parts,
        weights,
        preferred_element_type=F32,
    )
    single_out = (single_rep.astype(F32) + mixed_out).astype(BF)
    return (pair_out, single_out, bias_grad)


def solution(mesh):
    placed = (
        P("row", ("grp", "col"), None),
        P(),
        P(),
        P(),
        P(),
        P(),
        P(),
        P(),
        P("col", "row", None),
        P(None, None, "grp"),
        P("grp", None),
        P("col", "row", None),
    )

    return jax.shard_map(
        on_device,
        mesh=mesh,
        in_specs=placed,
        out_specs=(P("row", ("grp", "col"), None), P("col", "row", None), P("grp", "row", "col")),
        check_vma=False,
    )
```

```python
import math

import jax
import jax.numpy as jnp
from jax import lax
from jax.experimental import pallas as pl
from jax.experimental.pallas import tpu as pltpu
from jax.sharding import Mesh
from jax.sharding import PartitionSpec as P

BF = jnp.bfloat16
F32 = jnp.float32


def normalize(values, axis_at):
    average = jnp.mean(values, axis=axis_at, keepdims=True)
    centred = values - average
    variance = jnp.mean(centred * centred, axis=axis_at, keepdims=True)
    return centred * lax.rsqrt(variance + 1e-05)


SWAP = [(0, 1), (1, 0)]


def gather_grp(value, axis_at):
    far = lax.ppermute(value, "near", SWAP)
    both = jnp.concatenate([value, far], axis=axis_at)
    near = lax.ppermute(both, "core", SWAP)
    return jnp.concatenate([both, near], axis=axis_at)


def attention_kernel(
    heads,
    head_size,
    row_ref,
    qt_ref,
    dmt_ref,
    gt_ref,
    own_ref,
    last_ref,
    next_ref,
    top_ref,
    low_ref,
    bias_ref,
    gated_ref,
    grad_ref,
    k_s,
    v_s,
    qbd,
    dbd,
    st,
    dpt,
    pt,
    gacc,
):
    samples, width, rows = qt_ref.shape
    row_count = 4
    keys = rows * row_count
    scale = 1.0 / math.sqrt(head_size)
    row_at = row_ref[0]
    qbd[...] = jnp.zeros_like(qbd)
    dbd[...] = jnp.zeros_like(dbd)
    chunk = 64
    groups = chunk // 8

    def one_sample(s, unused):
        for step, halves in enumerate(
            (
                (own_ref.at[0], own_ref.at[1]),
                (last_ref.at[0], last_ref.at[1]),
                (top_ref, low_ref),
                (next_ref.at[0], next_ref.at[1]),
            )
        ):
            block = lax.rem(row_at + row_count - step, row_count)
            for n, ref in enumerate(halves):
                at = pl.multiple_of(block * rows + n * (rows // 2), rows // 2)
                k_s[pl.ds(at, rows // 2), :] = ref[s, :, 0:width]
                v_s[pl.ds(at, rows // 2), :] = ref[s, :, width : 2 * width]
        for h in range(heads):
            e0, i0 = h * head_size, h * rows
            qbd[e0 : e0 + head_size, i0 : i0 + rows] = qt_ref[s, e0 : e0 + head_size, :]
            dbd[e0 : e0 + head_size, i0 : i0 + rows] = dmt_ref[s, e0 : e0 + head_size, :]
        st[...] = jnp.dot(k_s[...], qbd[...], preferred_element_type=F32)
        dpt[...] = jnp.dot(v_s[...], dbd[...], preferred_element_type=F32)
        for h in range(heads):
            e0, i0 = h * head_size, h * rows
            lanes = slice(i0, i0 + rows)
            top = jnp.full((8, rows), -jnp.inf, F32)
            for b in range(keys // chunk):
                part = slice(b * chunk, (b + 1) * chunk)
                bias = bias_ref[b * groups : (b + 1) * groups, h, :, :].reshape(chunk, rows)
                x = st[part, lanes] * scale + bias
                st[part, lanes] = x
                top = jnp.maximum(top, jnp.max(x.reshape(groups, 8, rows), axis=0))
            peak = jnp.max(top, axis=0, keepdims=True)
            total = jnp.zeros((8, rows), F32)
            dots = jnp.zeros((8, rows), F32)
            for b in range(keys // chunk):
                part = slice(b * chunk, (b + 1) * chunk)
                w = jnp.exp(st[part, lanes] - peak)
                st[part, lanes] = w
                total = total + jnp.sum(w.reshape(groups, 8, rows), axis=0)
                dots = dots + jnp.sum((w * dpt[part, lanes]).reshape(groups, 8, rows), axis=0)
            inverse = 1.0 / jnp.sum(total, axis=0, keepdims=True)
            inner = jnp.sum(dots, axis=0, keepdims=True) * inverse
            for b in range(keys // chunk):
                part = slice(b * chunk, (b + 1) * chunk)
                p = st[part, lanes] * inverse
                pt[part, lanes] = p.astype(BF)
                d = p * (dpt[part, lanes] - inner)

                @pl.when(s == 0)
                def _():
                    gacc[h, part, :] = d

                @pl.when(s > 0)
                def _():
                    gacc[h, part, :] = gacc[h, part, :] + d

            mixed = lax.dot_general(
                v_s[...],
                pt[:, lanes],
                (((0,), (0,)), ((), ())),
                preferred_element_type=F32,
            )
            gated_ref[s, e0 : e0 + head_size, :] = (
                mixed[e0 : e0 + head_size, :] * gt_ref[s, e0 : e0 + head_size, :]
            ).astype(BF)
        return unused

    lax.fori_loop(0, samples, one_sample, 0)
    parts, _, width_j, _ = grad_ref.shape
    for h in range(heads):
        for c in range(parts):
            grad_ref[c, h, :, :] = gacc[h, c * width_j : (c + 1) * width_j, :].astype(BF)


def on_device(
    pair_rep,
    residue_index,
    chain_index,
    token_mask,
    relpos_table,
    proj_in,
    out_proj,
    bias_weight,
    single_rep,
    w_qkvg,
    w_out,
    cotangent,
):
    tok_rows, col_width, channels = pair_rep.shape
    col_count = lax.axis_size("col")
    near_count = lax.axis_size("near")
    core_count = lax.axis_size("core")
    grp_count = near_count * core_count
    row_count = lax.axis_size("row")
    row_at = lax.axis_index("row")
    core_at = lax.axis_index("core")
    grp_at = lax.axis_index("near") * core_count + core_at
    col_at = lax.axis_index("col")
    samples = single_rep.shape[0]
    head_width = w_out.shape[0]
    all_heads = bias_weight.shape[1]
    heads = all_heads // grp_count
    head_size = head_width // heads
    row_start = row_at * tok_rows
    col_start = (grp_at * col_count + col_at) * col_width
    table = jnp.stack([residue_index, chain_index, token_mask])
    of_rows = lax.dynamic_slice_in_dim(table, row_start, tok_rows, 1)
    of_cols = lax.dynamic_slice_in_dim(table, col_start, col_width, 1)
    mask_rows, mask_cols = of_rows[2], of_cols[2]

    normed_x = normalize(single_rep.astype(F32), 2).astype(BF)
    key_value = jnp.einsum(
        "srd,tde->srte", normed_x, w_qkvg[1:3], preferred_element_type=F32
    )
    keep_rows = (mask_rows == 1)[None, :, None, None]
    is_value = (jnp.arange(2) == 1)[None, None, :, None]
    key_value = jnp.where(keep_rows | is_value, key_value, 0.0).astype(BF)
    key_value = key_value.reshape(samples, 2, tok_rows // 2, 2 * head_width).transpose(1, 0, 2, 3)
    onward = [(i, (i + 1) % row_count) for i in range(row_count)]
    backward = [(i, (i + row_count - 1) % row_count) for i in range(row_count)]
    from_last = lax.ppermute(key_value, "row", onward)
    from_next = lax.ppermute(key_value, "row", backward)
    last_half, next_half = from_last[0], from_next[1]
    far_top = lax.ppermute(last_half, "row", onward)
    far_low = lax.ppermute(next_half, "row", backward)

    pair_tile = pair_rep.transpose(1, 0, 2).astype(F32)
    offsets = jnp.clip(of_rows[0][None, :] - of_cols[0][:, None], -32, 32) + 32
    bin_ids = jnp.where(of_rows[1][None, :] == of_cols[1][:, None], offsets, 65)
    onehot = (
        bin_ids[:, :, None] == jnp.arange(relpos_table.shape[0], dtype=jnp.int32)[None, None, :]
    ).astype(BF)
    pair_in = pair_tile + jnp.einsum(
        "jib,bc->jic", onehot, relpos_table, preferred_element_type=F32
    )
    normed = normalize(pair_in, 2).astype(BF)
    projected = jnp.einsum(
        "jic,ce->eji", normed, proj_in[:, : 4 * channels], preferred_element_type=F32
    )
    pair_mask = (mask_cols[:, None] * mask_rows[None, :]).astype(F32)[None]
    left_in = (
        jax.nn.sigmoid(projected[2 * channels : 3 * channels]) * projected[:channels] * pair_mask
    ).astype(BF)
    right_in = (
        jax.nn.sigmoid(projected[3 * channels :]) * projected[channels : 2 * channels] * pair_mask
    ).astype(BF)
    everywhere = ("row", "col", "near")
    count = row_count * col_count * near_count
    send = jnp.stack([left_in, right_in], axis=1).reshape(count, 2 * col_width, tok_rows)
    got = lax.all_to_all(send, everywhere, 0, 0, tiled=True)
    got = got.reshape(row_count, col_count, near_count, 2, col_width, tok_rows)
    left_own, right_own = got[:, :, :, 0], got[:, :, :, 1]
    left_other = lax.ppermute(left_own, "core", SWAP)
    first = core_at == 0
    left_all = (
        jnp.stack(
            [jnp.where(first, left_own, left_other), jnp.where(first, left_other, left_own)],
            axis=3,
        )
        .transpose(0, 2, 3, 1, 4, 5)
        .reshape(row_count, grp_count, tok_rows, tok_rows)
    )
    right_all = right_own.reshape(row_count, col_count * near_count * col_width, tok_rows)
    triangle = jnp.einsum("rgik,rjk->gji", left_all, right_all, preferred_element_type=F32)
    back = triangle.astype(BF).reshape(count, col_width, tok_rows)
    tri_local = lax.all_to_all(back, everywhere, 0, 0, tiled=True)
    tri_local = tri_local.reshape(channels, col_width, tok_rows)
    out_normed = normalize(tri_local.astype(F32), 0).astype(BF)
    gate_out = jax.nn.sigmoid(
        jnp.einsum("jic,cd->jid", normed, proj_in[:, 4 * channels :], preferred_element_type=F32)
    )
    update = jnp.einsum("cji,cd->jid", out_normed, out_proj, preferred_element_type=F32)
    pair_new = pair_in + gate_out * update
    pair_out = pair_new.astype(BF).transpose(1, 0, 2)
    bias_local = jnp.einsum(
        "jic,ch->hji", normalize(pair_new, 2), bias_weight, precision=lax.Precision.HIGHEST
    )
    bias_local = jnp.where((mask_cols == 1)[None, :, None], bias_local, -1000000000.0)
    copies = jnp.broadcast_to(
        bias_local.reshape(grp_count, 1, heads, col_width, tok_rows),
        (grp_count, col_count, heads, col_width, tok_rows),
    ).reshape(grp_count * col_count, heads, col_width, tok_rows)
    bias_all = lax.all_to_all(copies, ("near", "core", "col"), 0, 0, tiled=True)

    query_t = jnp.einsum("srd,de->ser", normed_x, w_qkvg[0], preferred_element_type=F32).astype(BF)
    gate_t = jax.nn.sigmoid(
        jnp.einsum("srd,de->ser", normed_x, w_qkvg[3], preferred_element_type=F32)
    )
    back_t = jnp.einsum("srd,ed->ser", cotangent, w_out, preferred_element_type=F32)
    d_mixed_t = (back_t * gate_t).astype(BF)
    weights = gather_grp(w_out, 0)
    keys = row_count * tok_rows
    vmem = pl.BlockSpec(memory_space=pltpu.VMEM)
    gated_t, grads = pl.pallas_call(
        lambda *refs: attention_kernel(heads, head_size, *refs),
        out_shape=(
            jax.ShapeDtypeStruct((samples, head_width, tok_rows), BF),
            jax.ShapeDtypeStruct((col_count, heads, keys // col_count, tok_rows), BF),
        ),
        in_specs=[pl.BlockSpec(memory_space=pltpu.SMEM)] + [vmem] * 9,
        out_specs=(vmem, vmem),
        scratch_shapes=[
            pltpu.VMEM((keys, head_width), BF),
            pltpu.VMEM((keys, head_width), BF),
            pltpu.VMEM((head_width, heads * tok_rows), BF),
            pltpu.VMEM((head_width, heads * tok_rows), BF),
            pltpu.VMEM((keys, heads * tok_rows), F32),
            pltpu.VMEM((keys, heads * tok_rows), F32),
            pltpu.VMEM((keys, heads * tok_rows), BF),
            pltpu.VMEM((heads, keys, tok_rows), F32),
        ],
        name="attention",
    )(
        row_at.astype(jnp.int32).reshape(1),
        query_t,
        d_mixed_t,
        gate_t,
        key_value,
        from_last,
        from_next,
        far_top,
        far_low,
        pltpu.with_memory_space_constraint(bias_all, pltpu.VMEM),
    )
    gated_parts = gather_grp(gated_t, 1)
    grad_parts = lax.all_to_all(grads, "col", 0, 0, tiled=True)
    grad_sum = jnp.sum(grad_parts.astype(F32), axis=0)
    bias_grad = grad_sum.transpose(0, 2, 1)
    mixed_out = jnp.einsum(
        "ser,ed->srd",
        gated_parts,
        weights,
        preferred_element_type=F32,
    )
    single_out = (single_rep.astype(F32) + mixed_out).astype(BF)
    return (pair_out, single_out, bias_grad)


def solution(mesh):
    grp, row, col = (mesh.shape[name] for name in ("grp", "row", "col"))
    split = Mesh(mesh.devices.reshape(grp // 2, 2, row, col), ("near", "core", "row", "col"))
    both = ("near", "core")
    placed = (
        P("row", (*both, "col"), None),
        P(),
        P(),
        P(),
        P(),
        P(),
        P(),
        P(),
        P("col", "row", None),
        P(None, None, both),
        P(both, None),
        P("col", "row", None),
    )

    return jax.shard_map(
        on_device,
        mesh=split,
        in_specs=placed,
        out_specs=(P("row", (*both, "col"), None), P("col", "row", None), P(both, "row", "col")),
        check_vma=False,
    )
```

```python
import math

import jax
import jax.numpy as jnp
from jax import lax
from jax.experimental import pallas as pl
from jax.experimental.pallas import tpu as pltpu
from jax.sharding import Mesh
from jax.sharding import PartitionSpec as P

BF = jnp.bfloat16
F32 = jnp.float32
LOG2E = 1.4426950408889634
HIDDEN = -65504.0


def normalize(values, axis_at):
    average = jnp.mean(values, axis=axis_at, keepdims=True)
    centred = values - average
    variance = jnp.mean(centred * centred, axis=axis_at, keepdims=True)
    return centred * lax.rsqrt(variance + 1e-05)


SWAP = [(0, 1), (1, 0)]


def gather_grp(value, axis_at):
    far = lax.ppermute(value, "near", SWAP)
    both = jnp.concatenate([value, far], axis=axis_at)
    near = lax.ppermute(both, "core", SWAP)
    return jnp.concatenate([both, near], axis=axis_at)


def attention_kernel(
    heads,
    head_size,
    row_ref,
    qt_ref,
    dmt_ref,
    gt_ref,
    own_ref,
    last_ref,
    next_ref,
    top_ref,
    low_ref,
    bias_ref,
    gated_ref,
    grad_ref,
    k_s,
    v_s,
    qbd,
    dbd,
    st,
    dpt,
    pt,
    gacc,
):
    samples, width, rows = qt_ref.shape
    row_count = 4
    scale = LOG2E / math.sqrt(head_size)
    row_at = row_ref[0]
    qbd[...] = jnp.zeros_like(qbd)
    dbd[...] = jnp.zeros_like(dbd)
    gacc[...] = jnp.zeros_like(gacc)
    tiles = rows // 8

    def fold(x, op):
        return op(x.reshape(tiles, 8, 2 * rows), axis=0)

    def one_sample(s, unused):
        for step, halves in enumerate(
            (
                (own_ref.at[0], own_ref.at[1]),
                (last_ref.at[0], last_ref.at[1]),
                (top_ref, low_ref),
                (next_ref.at[0], next_ref.at[1]),
            )
        ):
            block = lax.rem(row_at + row_count - step, row_count)
            for n, ref in enumerate(halves):
                at = pl.multiple_of(block * rows + n * (rows // 2), rows // 2)
                k_s[pl.ds(at, rows // 2), :] = ref[s, :, 0:width]
                v_s[pl.ds(at, rows // 2), :] = ref[s, :, width : 2 * width]
        for h in range(heads):
            e0, i0 = h * head_size, h * rows
            qbd[e0 : e0 + head_size, i0 : i0 + rows] = qt_ref[s, e0 : e0 + head_size, :]
            dbd[e0 : e0 + head_size, i0 : i0 + rows] = dmt_ref[s, e0 : e0 + head_size, :]
        for h in range(0, heads, 2):
            lanes = slice(h * rows, (h + 2) * rows)
            top = jnp.full((8, 2 * rows), -jnp.inf, F32)
            for b in range(row_count):
                part = slice(b * rows, (b + 1) * rows)
                places = slice(b * tiles, (b + 1) * tiles)
                bias = jnp.concatenate(
                    [bias_ref[places, h + n, :, :].reshape(rows, rows) for n in range(2)], axis=1
                )
                x = jnp.dot(k_s[part, :], qbd[:, lanes], preferred_element_type=F32)
                x = x * scale + bias
                st[part, lanes] = x
                top = jnp.maximum(top, fold(x, jnp.max))
            peak = jnp.max(top, axis=0, keepdims=True)
            total = jnp.zeros((8, 2 * rows), F32)
            dots = jnp.zeros((8, 2 * rows), F32)
            for b in range(row_count):
                part = slice(b * rows, (b + 1) * rows)
                d = jnp.dot(v_s[part, :], dbd[:, lanes], preferred_element_type=F32)
                w = jnp.exp2(st[part, lanes] - peak)
                st[part, lanes] = w
                dpt[part, lanes] = d
                total = total + fold(w, jnp.sum)
                dots = dots + fold(w * d, jnp.sum)
            inverse = 1.0 / jnp.sum(total, axis=0, keepdims=True)
            inner = jnp.sum(dots, axis=0, keepdims=True) * inverse
            for b in range(row_count):
                part = slice(b * rows, (b + 1) * rows)
                p = st[part, lanes] * inverse
                pt[part, lanes] = p.astype(BF)
                gacc[part, lanes] = gacc[part, lanes] + p * (dpt[part, lanes] - inner)
        mixed = lax.dot_general(
            v_s[...], pt[...], (((0,), (0,)), ((), ())), preferred_element_type=F32
        )
        for h in range(heads):
            e0, i0 = h * head_size, h * rows
            gated_ref[s, e0 : e0 + head_size, :] = (
                mixed[e0 : e0 + head_size, i0 : i0 + rows] * gt_ref[s, e0 : e0 + head_size, :]
            ).astype(BF)
        return unused

    lax.fori_loop(0, samples, one_sample, 0)
    parts, _, width_j, _ = grad_ref.shape
    for h in range(heads):
        for c in range(parts):
            grad_ref[c, h, :, :] = gacc[
                c * width_j : (c + 1) * width_j, h * rows : (h + 1) * rows
            ].astype(BF)


def on_device(
    pair_rep,
    residue_index,
    chain_index,
    token_mask,
    relpos_table,
    proj_in,
    out_proj,
    bias_weight,
    single_rep,
    w_qkvg,
    w_out,
    cotangent,
):
    tok_rows, col_width, channels = pair_rep.shape
    col_count = lax.axis_size("col")
    near_count = lax.axis_size("near")
    core_count = lax.axis_size("core")
    grp_count = near_count * core_count
    row_count = lax.axis_size("row")
    row_at = lax.axis_index("row")
    core_at = lax.axis_index("core")
    grp_at = lax.axis_index("near") * core_count + core_at
    col_at = lax.axis_index("col")
    samples = single_rep.shape[0]
    head_width = w_out.shape[0]
    all_heads = bias_weight.shape[1]
    heads = all_heads // grp_count
    head_size = head_width // heads
    row_start = row_at * tok_rows
    col_start = (grp_at * col_count + col_at) * col_width
    table = jnp.stack([residue_index, chain_index, token_mask])
    of_rows = lax.dynamic_slice_in_dim(table, row_start, tok_rows, 1)
    of_cols = lax.dynamic_slice_in_dim(table, col_start, col_width, 1)
    mask_rows, mask_cols = of_rows[2], of_cols[2]

    normed_x = normalize(single_rep.astype(F32), 2).astype(BF)
    key_value = jnp.einsum(
        "srd,tde->srte", normed_x, w_qkvg[1:3], preferred_element_type=F32
    )
    keep_rows = (mask_rows == 1)[None, :, None, None]
    is_value = (jnp.arange(2) == 1)[None, None, :, None]
    key_value = jnp.where(keep_rows | is_value, key_value, 0.0).astype(BF)
    key_value = key_value.reshape(samples, 2, tok_rows // 2, 2 * head_width).transpose(1, 0, 2, 3)
    onward = [(i, (i + 1) % row_count) for i in range(row_count)]
    backward = [(i, (i + row_count - 1) % row_count) for i in range(row_count)]
    from_last = lax.ppermute(key_value, "row", onward)
    from_next = lax.ppermute(key_value, "row", backward)
    last_half, next_half = from_last[0], from_next[1]
    far_top = lax.ppermute(last_half, "row", onward)
    far_low = lax.ppermute(next_half, "row", backward)

    pair_tile = pair_rep.transpose(1, 0, 2).astype(F32)
    offsets = jnp.clip(of_rows[0][None, :] - of_cols[0][:, None], -32, 32) + 32
    bin_ids = jnp.where(of_rows[1][None, :] == of_cols[1][:, None], offsets, 65)
    onehot = (
        bin_ids[:, :, None] == jnp.arange(relpos_table.shape[0], dtype=jnp.int32)[None, None, :]
    ).astype(BF)
    pair_in = pair_tile + jnp.einsum(
        "jib,bc->jic", onehot, relpos_table, preferred_element_type=F32
    )
    normed = normalize(pair_in, 2).astype(BF)
    projected = jnp.einsum(
        "jic,ce->eji", normed, proj_in[:, : 4 * channels], preferred_element_type=F32
    )
    pair_mask = (mask_cols[:, None] * mask_rows[None, :]).astype(F32)[None]
    left_in = (
        jax.nn.sigmoid(projected[2 * channels : 3 * channels]) * projected[:channels] * pair_mask
    ).astype(BF)
    right_in = (
        jax.nn.sigmoid(projected[3 * channels :]) * projected[channels : 2 * channels] * pair_mask
    ).astype(BF)
    everywhere = ("row", "col", "near")
    count = row_count * col_count * near_count
    send = jnp.stack([left_in, right_in], axis=1).reshape(count, 2 * col_width, tok_rows)
    got = lax.all_to_all(send, everywhere, 0, 0, tiled=True)
    got = got.reshape(row_count, col_count, near_count, 2, col_width, tok_rows)
    left_own, right_own = got[:, :, :, 0], got[:, :, :, 1]
    left_other = lax.ppermute(left_own, "core", SWAP)
    first = core_at == 0
    left_all = (
        jnp.stack(
            [jnp.where(first, left_own, left_other), jnp.where(first, left_other, left_own)],
            axis=3,
        )
        .transpose(0, 2, 3, 1, 4, 5)
        .reshape(row_count, grp_count, tok_rows, tok_rows)
    )
    right_all = right_own.reshape(row_count, col_count * near_count * col_width, tok_rows)
    triangle = jnp.einsum("rgik,rjk->gji", left_all, right_all, preferred_element_type=F32)
    back = triangle.astype(BF).reshape(count, col_width, tok_rows)
    tri_local = lax.all_to_all(back, everywhere, 0, 0, tiled=True)
    tri_local = tri_local.reshape(channels, col_width, tok_rows)
    out_normed = normalize(tri_local.astype(F32), 0).astype(BF)
    bias_scaled = lax.optimization_barrier(bias_weight * LOG2E)
    gate_out = jax.nn.sigmoid(
        jnp.einsum("jic,cd->jid", normed, proj_in[:, 4 * channels :], preferred_element_type=F32)
    )
    update = jnp.einsum("cji,cd->jid", out_normed, out_proj, preferred_element_type=F32)
    pair_new = pair_in + gate_out * update
    pair_out = pair_new.astype(BF).transpose(1, 0, 2)
    bias_local = jnp.einsum(
        "jic,ch->hji", normalize(pair_new, 2), bias_scaled, precision=lax.Precision.HIGHEST
    )
    bias_local = jnp.where((mask_cols == 1)[None, :, None], bias_local, HIDDEN).astype(jnp.float16)
    copies = jnp.broadcast_to(
        bias_local.reshape(grp_count, 1, heads, col_width, tok_rows),
        (grp_count, col_count, heads, col_width, tok_rows),
    ).reshape(grp_count * col_count, heads, col_width, tok_rows)
    bias_all = lax.all_to_all(copies, ("near", "core", "col"), 0, 0, tiled=True)
    bias_all = bias_all.astype(F32)
    bias_all = jnp.where(bias_all > 0.5 * HIDDEN, bias_all, -1000000000.0 * LOG2E)

    query_t = jnp.einsum("srd,de->ser", normed_x, w_qkvg[0], preferred_element_type=F32).astype(BF)
    gate_t = jax.nn.sigmoid(
        jnp.einsum("srd,de->ser", normed_x, w_qkvg[3], preferred_element_type=F32)
    )
    back_t = jnp.einsum("srd,ed->ser", cotangent, w_out, preferred_element_type=F32)
    d_mixed_t = (back_t * gate_t).astype(BF)
    weights = gather_grp(w_out, 0)
    keys = row_count * tok_rows
    vmem = pl.BlockSpec(memory_space=pltpu.VMEM)
    gated_t, grads = pl.pallas_call(
        lambda *refs: attention_kernel(heads, head_size, *refs),
        out_shape=(
            jax.ShapeDtypeStruct((samples, head_width, tok_rows), BF),
            jax.ShapeDtypeStruct((col_count, heads, keys // col_count, tok_rows), BF),
        ),
        in_specs=[pl.BlockSpec(memory_space=pltpu.SMEM)] + [vmem] * 9,
        out_specs=(vmem, vmem),
        scratch_shapes=[
            pltpu.VMEM((keys, head_width), BF),
            pltpu.VMEM((keys, head_width), BF),
            pltpu.VMEM((head_width, heads * tok_rows), BF),
            pltpu.VMEM((head_width, heads * tok_rows), BF),
            pltpu.VMEM((keys, heads * tok_rows), F32),
            pltpu.VMEM((keys, heads * tok_rows), F32),
            pltpu.VMEM((keys, heads * tok_rows), BF),
            pltpu.VMEM((keys, heads * tok_rows), F32),
        ],
        name="attention",
    )(
        row_at.astype(jnp.int32).reshape(1),
        query_t,
        d_mixed_t,
        gate_t,
        key_value,
        from_last,
        from_next,
        far_top,
        far_low,
        pltpu.with_memory_space_constraint(bias_all, pltpu.VMEM),
    )
    gated_parts = gather_grp(gated_t, 1)
    grad_parts = lax.all_to_all(grads, "col", 0, 0, tiled=True)
    grad_sum = jnp.sum(grad_parts.astype(F32), axis=0)
    bias_grad = grad_sum.transpose(0, 2, 1)
    mixed_out = jnp.einsum(
        "ser,ed->srd",
        gated_parts,
        weights,
        preferred_element_type=F32,
    )
    single_out = (single_rep.astype(F32) + mixed_out).astype(BF)
    return (pair_out, single_out, bias_grad)


def solution(mesh):
    grp, row, col = (mesh.shape[name] for name in ("grp", "row", "col"))
    split = Mesh(mesh.devices.reshape(grp // 2, 2, row, col), ("near", "core", "row", "col"))
    both = ("near", "core")
    placed = (
        P("row", (*both, "col"), None),
        P(),
        P(),
        P(),
        P(),
        P(),
        P(),
        P(),
        P("col", "row", None),
        P(None, None, both),
        P(both, None),
        P("col", "row", None),
    )

    return jax.shard_map(
        on_device,
        mesh=split,
        in_specs=placed,
        out_specs=(P("row", (*both, "col"), None), P("col", "row", None), P(both, "row", "col")),
        check_vma=False,
    )
```

```python
import math

import jax
import jax.numpy as jnp
from jax import lax
from jax.experimental import pallas as pl
from jax.experimental.pallas import tpu as pltpu
from jax.sharding import Mesh
from jax.sharding import PartitionSpec as P

BF = jnp.bfloat16
F32 = jnp.float32
LOG2E = 1.4426950408889634
HIDDEN = -65504.0


def normalize(values, axis_at):
    average = jnp.mean(values, axis=axis_at, keepdims=True)
    centred = values - average
    variance = jnp.mean(centred * centred, axis=axis_at, keepdims=True)
    return centred * lax.rsqrt(variance + 1e-05)


SWAP = [(0, 1), (1, 0)]


def gather_grp(value, axis_at):
    far = lax.ppermute(value, "near", SWAP)
    both = jnp.concatenate([value, far], axis=axis_at)
    near = lax.ppermute(both, "core", SWAP)
    return jnp.concatenate([both, near], axis=axis_at)


def attention_kernel(
    heads,
    head_size,
    row_ref,
    qt_ref,
    dmt_ref,
    gt_ref,
    own_ref,
    last_ref,
    next_ref,
    top_ref,
    low_ref,
    bias_ref,
    gated_ref,
    grad_ref,
    k_s,
    v_s,
    qbd,
    dbd,
    st,
    dpt,
    pt,
    gacc,
):
    _, width, rows = qt_ref.shape
    samples = top_ref.shape[0]
    row_count = 4
    scale = LOG2E / math.sqrt(head_size)
    row_at = row_ref[0]
    s = pl.program_id(0)

    @pl.when(s == 0)
    def _():
        qbd[...] = jnp.zeros_like(qbd)
        dbd[...] = jnp.zeros_like(dbd)
        gacc[...] = jnp.zeros_like(gacc)

    tiles = rows // 8

    def fold(x, op):
        return op(x.reshape(tiles, 8, 2 * rows), axis=0)

    for step, halves in enumerate(
        (
            (own_ref.at[0, 0], own_ref.at[1, 0]),
            (last_ref.at[0, 0], last_ref.at[1, 0]),
            (top_ref.at[s], low_ref.at[s]),
            (next_ref.at[0, 0], next_ref.at[1, 0]),
        )
    ):
        block = lax.rem(row_at + row_count - step, row_count)
        for n, ref in enumerate(halves):
            at = pl.multiple_of(block * rows + n * (rows // 2), rows // 2)
            k_s[pl.ds(at, rows // 2), :] = ref[:, 0:width]
            v_s[pl.ds(at, rows // 2), :] = ref[:, width : 2 * width]
    for h in range(heads):
        e0, i0 = h * head_size, h * rows
        qbd[e0 : e0 + head_size, i0 : i0 + rows] = qt_ref[0, e0 : e0 + head_size, :]
        dbd[e0 : e0 + head_size, i0 : i0 + rows] = dmt_ref[0, e0 : e0 + head_size, :]
    for h in range(0, heads, 2):
        lanes = slice(h * rows, (h + 2) * rows)
        top = jnp.full((8, 2 * rows), -jnp.inf, F32)
        for b in range(row_count):
            part = slice(b * rows, (b + 1) * rows)
            places = slice(b * tiles, (b + 1) * tiles)
            bias = jnp.concatenate(
                [bias_ref[places, h + n, :, :].reshape(rows, rows) for n in range(2)], axis=1
            )
            x = jnp.dot(k_s[part, :], qbd[:, lanes], preferred_element_type=F32)
            x = x * scale + bias
            st[part, lanes] = x
            top = jnp.maximum(top, fold(x, jnp.max))
        peak = jnp.max(top, axis=0, keepdims=True)
        total = jnp.zeros((8, 2 * rows), F32)
        dots = jnp.zeros((8, 2 * rows), F32)
        for b in range(row_count):
            part = slice(b * rows, (b + 1) * rows)
            d = jnp.dot(v_s[part, :], dbd[:, lanes], preferred_element_type=F32)
            w = jnp.exp2(st[part, lanes] - peak)
            st[part, lanes] = w
            dpt[part, lanes] = d
            total = total + fold(w, jnp.sum)
            dots = dots + fold(w * d, jnp.sum)
        inverse = 1.0 / jnp.sum(total, axis=0, keepdims=True)
        inner = jnp.sum(dots, axis=0, keepdims=True) * inverse
        for b in range(row_count):
            part = slice(b * rows, (b + 1) * rows)
            p = st[part, lanes] * inverse
            pt[part, lanes] = p.astype(BF)
            gacc[part, lanes] = gacc[part, lanes] + p * (dpt[part, lanes] - inner)
    mixed = lax.dot_general(
        v_s[...], pt[...], (((0,), (0,)), ((), ())), preferred_element_type=F32
    )
    for h in range(heads):
        e0, i0 = h * head_size, h * rows
        gated_ref[0, e0 : e0 + head_size, :] = (
            mixed[e0 : e0 + head_size, i0 : i0 + rows] * gt_ref[0, e0 : e0 + head_size, :]
        ).astype(BF)

    @pl.when(s == samples - 1)
    def _():
        parts, _, width_j, _ = grad_ref.shape
        for h in range(heads):
            for c in range(parts):
                grad_ref[c, h, :, :] = gacc[
                    c * width_j : (c + 1) * width_j, h * rows : (h + 1) * rows
                ].astype(BF)


def on_device(
    pair_rep,
    residue_index,
    chain_index,
    token_mask,
    relpos_table,
    proj_in,
    out_proj,
    bias_weight,
    single_rep,
    w_qkvg,
    w_out,
    cotangent,
):
    tok_rows, col_width, channels = pair_rep.shape
    col_count = lax.axis_size("col")
    near_count = lax.axis_size("near")
    core_count = lax.axis_size("core")
    grp_count = near_count * core_count
    row_count = lax.axis_size("row")
    row_at = lax.axis_index("row")
    core_at = lax.axis_index("core")
    grp_at = lax.axis_index("near") * core_count + core_at
    col_at = lax.axis_index("col")
    samples = single_rep.shape[0]
    head_width = w_out.shape[0]
    all_heads = bias_weight.shape[1]
    heads = all_heads // grp_count
    head_size = head_width // heads
    row_start = row_at * tok_rows
    col_start = (grp_at * col_count + col_at) * col_width
    table = jnp.stack([residue_index, chain_index, token_mask])
    of_rows = lax.dynamic_slice_in_dim(table, row_start, tok_rows, 1)
    of_cols = lax.dynamic_slice_in_dim(table, col_start, col_width, 1)
    mask_rows, mask_cols = of_rows[2], of_cols[2]

    normed_x = normalize(single_rep.astype(F32), 2).astype(BF)
    key_value = jnp.einsum(
        "srd,tde->srte", normed_x, w_qkvg[1:3], preferred_element_type=F32
    )
    keep_rows = (mask_rows == 1)[None, :, None, None]
    is_value = (jnp.arange(2) == 1)[None, None, :, None]
    key_value = jnp.where(keep_rows | is_value, key_value, 0.0).astype(BF)
    key_value = key_value.reshape(samples, 2, tok_rows // 2, 2 * head_width).transpose(1, 0, 2, 3)
    onward = [(i, (i + 1) % row_count) for i in range(row_count)]
    backward = [(i, (i + row_count - 1) % row_count) for i in range(row_count)]
    from_last = lax.ppermute(key_value, "row", onward)
    from_next = lax.ppermute(key_value, "row", backward)
    last_half, next_half = from_last[0], from_next[1]
    far_top = lax.ppermute(last_half, "row", onward)
    far_low = lax.ppermute(next_half, "row", backward)

    pair_tile = pair_rep.transpose(1, 0, 2).astype(F32)
    offsets = jnp.clip(of_rows[0][None, :] - of_cols[0][:, None], -32, 32) + 32
    bin_ids = jnp.where(of_rows[1][None, :] == of_cols[1][:, None], offsets, 65)
    onehot = (
        bin_ids[:, :, None] == jnp.arange(relpos_table.shape[0], dtype=jnp.int32)[None, None, :]
    ).astype(BF)
    pair_in = pair_tile + jnp.einsum(
        "jib,bc->jic", onehot, relpos_table, preferred_element_type=F32
    )
    normed = normalize(pair_in, 2).astype(BF)
    projected = jnp.einsum(
        "jic,ce->eji", normed, proj_in[:, : 4 * channels], preferred_element_type=F32
    )
    pair_mask = (mask_cols[:, None] * mask_rows[None, :]).astype(F32)[None]
    left_in = (
        jax.nn.sigmoid(projected[2 * channels : 3 * channels]) * projected[:channels] * pair_mask
    ).astype(BF)
    right_in = (
        jax.nn.sigmoid(projected[3 * channels :]) * projected[channels : 2 * channels] * pair_mask
    ).astype(BF)
    everywhere = ("row", "col", "near")
    count = row_count * col_count * near_count
    send = jnp.stack([left_in, right_in], axis=1).reshape(count, 2 * col_width, tok_rows)
    got = lax.all_to_all(send, everywhere, 0, 0, tiled=True)
    got = got.reshape(row_count, col_count, near_count, 2, col_width, tok_rows)
    left_own, right_own = got[:, :, :, 0], got[:, :, :, 1]
    left_other = lax.ppermute(left_own, "core", SWAP)
    first = core_at == 0
    left_all = (
        jnp.stack(
            [jnp.where(first, left_own, left_other), jnp.where(first, left_other, left_own)],
            axis=3,
        )
        .transpose(0, 2, 3, 1, 4, 5)
        .reshape(row_count, grp_count, tok_rows, tok_rows)
    )
    right_all = right_own.reshape(row_count, col_count * near_count * col_width, tok_rows)
    triangle = jnp.einsum("rgik,rjk->gji", left_all, right_all, preferred_element_type=F32)
    back = triangle.astype(BF).reshape(count, col_width, tok_rows)
    tri_local = lax.all_to_all(back, everywhere, 0, 0, tiled=True)
    tri_local = tri_local.reshape(channels, col_width, tok_rows)
    out_normed = normalize(tri_local.astype(F32), 0).astype(BF)
    bias_scaled = lax.optimization_barrier(bias_weight * LOG2E)
    key_tile = lax.optimization_barrier(
        jnp.broadcast_to((mask_cols == 1).astype(F32)[:, None], (col_width, tok_rows))
    )
    gate_out = jax.nn.sigmoid(
        jnp.einsum("jic,cd->jid", normed, proj_in[:, 4 * channels :], preferred_element_type=F32)
    )
    update = jnp.einsum("cji,cd->jid", out_normed, out_proj, preferred_element_type=F32)
    pair_new = pair_in + gate_out * update
    pair_out = pair_new.astype(BF).transpose(1, 0, 2)
    bias_local = jnp.einsum(
        "jic,ch->hji", normalize(pair_new, 2), bias_scaled, precision=lax.Precision.HIGHEST
    )
    bias_local = jnp.where(key_tile[None] > 0.5, bias_local, HIDDEN).astype(jnp.float16)
    copies = jnp.broadcast_to(
        bias_local.reshape(grp_count, 1, heads, col_width, tok_rows),
        (grp_count, col_count, heads, col_width, tok_rows),
    ).reshape(grp_count * col_count, heads, col_width, tok_rows)
    bias_all = lax.all_to_all(copies, ("near", "core", "col"), 0, 0, tiled=True)
    bias_all = bias_all.astype(F32)
    bias_all = jnp.where(bias_all > 0.5 * HIDDEN, bias_all, -1000000000.0 * LOG2E)

    query_t = jnp.einsum("srd,de->ser", normed_x, w_qkvg[0], preferred_element_type=F32).astype(BF)
    gate_t = jax.nn.sigmoid(
        jnp.einsum("srd,de->ser", normed_x, w_qkvg[3], preferred_element_type=F32)
    )
    back_t = jnp.einsum("srd,ed->ser", cotangent, w_out, preferred_element_type=F32)
    d_mixed_t = (back_t * gate_t).astype(BF)
    weights = gather_grp(w_out, 0)
    keys = row_count * tok_rows
    vmem = pl.BlockSpec(memory_space=pltpu.VMEM)
    by_sample = pl.BlockSpec((1, head_width, tok_rows), lambda s: (s, 0, 0))
    of_tokens = pl.BlockSpec((2, 1, tok_rows // 2, 2 * head_width), lambda s: (0, s, 0, 0))
    gated_t, grads = pl.pallas_call(
        lambda *refs: attention_kernel(heads, head_size, *refs),
        out_shape=(
            pltpu.VMEM((samples, head_width, tok_rows), BF),
            pltpu.VMEM((col_count, heads, keys // col_count, tok_rows), BF),
        ),
        compiler_params=pltpu.CompilerParams(
            vmem_limit_bytes=24 << 20, dimension_semantics=("arbitrary",)
        ),
        grid=(samples,),
        in_specs=[pl.BlockSpec(memory_space=pltpu.SMEM)]
        + [by_sample] * 3
        + [of_tokens] * 3
        + [vmem] * 3,
        out_specs=(by_sample, vmem),
        scratch_shapes=[
            pltpu.VMEM((keys, head_width), BF),
            pltpu.VMEM((keys, head_width), BF),
            pltpu.VMEM((head_width, heads * tok_rows), BF),
            pltpu.VMEM((head_width, heads * tok_rows), BF),
            pltpu.VMEM((keys, heads * tok_rows), F32),
            pltpu.VMEM((keys, heads * tok_rows), F32),
            pltpu.VMEM((keys, heads * tok_rows), BF),
            pltpu.VMEM((keys, heads * tok_rows), F32),
        ],
        name="attention",
    )(
        row_at.astype(jnp.int32).reshape(1),
        *[
            pltpu.with_memory_space_constraint(value, pltpu.HBM)
            for value in (
                query_t,
                d_mixed_t,
                gate_t,
                key_value,
                from_last,
                from_next,
            )
        ],
        pltpu.with_memory_space_constraint(far_top, pltpu.VMEM),
        pltpu.with_memory_space_constraint(far_low, pltpu.VMEM),
        pltpu.with_memory_space_constraint(bias_all, pltpu.VMEM),
    )
    gated_parts = gather_grp(gated_t, 1)
    grad_parts = lax.all_to_all(grads, "col", 0, 0, tiled=True)
    grad_sum = jnp.sum(grad_parts.astype(F32), axis=0)
    bias_grad = grad_sum.transpose(0, 2, 1)
    mixed_out = jnp.einsum(
        "ser,ed->srd",
        gated_parts,
        weights,
        preferred_element_type=F32,
    )
    single_out = (single_rep.astype(F32) + mixed_out).astype(BF)
    return (pair_out, single_out, bias_grad)


def solution(mesh):
    grp, row, col = (mesh.shape[name] for name in ("grp", "row", "col"))
    split = Mesh(mesh.devices.reshape(grp // 2, 2, row, col), ("near", "core", "row", "col"))
    both = ("near", "core")
    placed = (
        P("row", (*both, "col"), None),
        P(),
        P(),
        P(),
        P(),
        P(),
        P(),
        P(),
        P("col", "row", None),
        P(None, None, both),
        P(both, None),
        P("col", "row", None),
    )

    return jax.shard_map(
        on_device,
        mesh=split,
        in_specs=placed,
        out_specs=(P("row", (*both, "col"), None), P("col", "row", None), P(both, "row", "col")),
        check_vma=False,
    )
```

```python
import math

import jax
import jax.numpy as jnp
from jax import lax
from jax.experimental import pallas as pl
from jax.experimental.pallas import tpu as pltpu
from jax.sharding import Mesh
from jax.sharding import PartitionSpec as P

BF = jnp.bfloat16
F32 = jnp.float32
LOG2E = 1.4426950408889634
HIDDEN = -65504.0


def normalize(values, axis_at):
    average = jnp.mean(values, axis=axis_at, keepdims=True)
    centred = values - average
    variance = jnp.mean(centred * centred, axis=axis_at, keepdims=True)
    return centred * lax.rsqrt(variance + 1e-05)


SWAP = [(0, 1), (1, 0)]


def gather_grp(value, axis_at):
    far = lax.ppermute(value, "near", SWAP)
    both = jnp.concatenate([value, far], axis=axis_at)
    near = lax.ppermute(both, "core", SWAP)
    return jnp.concatenate([both, near], axis=axis_at)


def attention_kernel(
    heads,
    head_size,
    row_ref,
    qt_ref,
    dmt_ref,
    gt_ref,
    own_ref,
    last_ref,
    next_ref,
    top_ref,
    low_ref,
    bias_ref,
    gated_ref,
    grad_ref,
    k_s,
    v_s,
    qbd,
    dbd,
    st,
    dpt,
    pt,
    gacc,
):
    _, width, rows = qt_ref.shape
    samples = top_ref.shape[0]
    row_count = 4
    scale = LOG2E / math.sqrt(head_size)
    row_at = row_ref[0]
    s = pl.program_id(0)

    @pl.when(s == 0)
    def _():
        qbd[...] = jnp.zeros_like(qbd)
        dbd[...] = jnp.zeros_like(dbd)
        gacc[...] = jnp.zeros_like(gacc)

    tiles = rows // 8

    def fold(x, op):
        return op(x.reshape(tiles, 8, 2 * rows), axis=0)

    for step, halves in enumerate(
        (
            (own_ref.at[0, 0], own_ref.at[1, 0]),
            (last_ref.at[0, 0], last_ref.at[1, 0]),
            (top_ref.at[s], low_ref.at[s]),
            (next_ref.at[0, 0], next_ref.at[1, 0]),
        )
    ):
        block = lax.rem(row_at + row_count - step, row_count)
        for n, ref in enumerate(halves):
            at = pl.multiple_of(block * rows + n * (rows // 2), rows // 2)
            k_s[pl.ds(at, rows // 2), :] = ref[:, 0:width]
            v_s[pl.ds(at, rows // 2), :] = ref[:, width : 2 * width]
    for h in range(heads):
        e0, i0 = h * head_size, h * rows
        qbd[e0 : e0 + head_size, i0 : i0 + rows] = qt_ref[0, e0 : e0 + head_size, :]
        dbd[e0 : e0 + head_size, i0 : i0 + rows] = dmt_ref[0, e0 : e0 + head_size, :]
    for h in range(0, heads, 2):
        lanes = slice(h * rows, (h + 2) * rows)
        top = jnp.full((8, 2 * rows), -jnp.inf, F32)
        for b in range(row_count):
            part = slice(b * rows, (b + 1) * rows)
            places = slice(b * tiles, (b + 1) * tiles)
            bias = jnp.concatenate(
                [bias_ref[places, h + n, :, :].reshape(rows, rows) for n in range(2)], axis=1
            )
            x = jnp.dot(k_s[part, :], qbd[:, lanes], preferred_element_type=F32)
            x = x * scale + bias
            st[part, lanes] = x
            top = jnp.maximum(top, fold(x, jnp.max))
        peak = jnp.max(top, axis=0, keepdims=True)
        total = jnp.zeros((8, 2 * rows), F32)
        dots = jnp.zeros((8, 2 * rows), F32)
        for b in range(row_count):
            part = slice(b * rows, (b + 1) * rows)
            d = jnp.dot(v_s[part, :], dbd[:, lanes], preferred_element_type=F32)
            w = jnp.exp2(st[part, lanes] - peak)
            st[part, lanes] = w
            dpt[part, lanes] = d
            total = total + fold(w, jnp.sum)
            dots = dots + fold(w * d, jnp.sum)
        inverse = 1.0 / jnp.sum(total, axis=0, keepdims=True)
        inner = jnp.sum(dots, axis=0, keepdims=True) * inverse
        for b in range(row_count):
            part = slice(b * rows, (b + 1) * rows)
            p = st[part, lanes] * inverse
            pt[part, lanes] = p.astype(BF)
            gacc[part, lanes] = gacc[part, lanes] + p * (dpt[part, lanes] - inner)
    mixed = lax.dot_general(
        v_s[...], pt[...], (((0,), (0,)), ((), ())), preferred_element_type=F32
    )
    for h in range(heads):
        e0, i0 = h * head_size, h * rows
        gated_ref[0, e0 : e0 + head_size, :] = (
            mixed[e0 : e0 + head_size, i0 : i0 + rows] * gt_ref[0, e0 : e0 + head_size, :]
        ).astype(BF)

    @pl.when(s == samples - 1)
    def _():
        parts, _, width_j, _ = grad_ref.shape
        for h in range(heads):
            for c in range(parts):
                grad_ref[c, h, :, :] = gacc[
                    c * width_j : (c + 1) * width_j, h * rows : (h + 1) * rows
                ].astype(BF)


def on_device(
    pair_rep,
    residue_index,
    chain_index,
    token_mask,
    relpos_table,
    proj_in,
    out_proj,
    bias_weight,
    single_rep,
    w_qkvg,
    w_out,
    cotangent,
):
    tok_rows, col_width, channels = pair_rep.shape
    col_count = lax.axis_size("col")
    near_count = lax.axis_size("near")
    core_count = lax.axis_size("core")
    grp_count = near_count * core_count
    row_count = lax.axis_size("row")
    row_at = lax.axis_index("row")
    core_at = lax.axis_index("core")
    grp_at = lax.axis_index("near") * core_count + core_at
    col_at = lax.axis_index("col")
    samples = single_rep.shape[0]
    head_width = w_out.shape[0]
    all_heads = bias_weight.shape[1]
    heads = all_heads // grp_count
    head_size = head_width // heads
    row_start = row_at * tok_rows
    col_start = (grp_at * col_count + col_at) * col_width
    table = jnp.stack([residue_index, chain_index, token_mask])
    of_rows = lax.dynamic_slice_in_dim(table, row_start, tok_rows, 1)
    of_cols = lax.dynamic_slice_in_dim(table, col_start, col_width, 1)
    mask_rows, mask_cols = of_rows[2], of_cols[2]

    normed_x = normalize(single_rep.astype(F32), 2).astype(BF)
    key_value = jnp.einsum(
        "srd,tde->srte", normed_x, w_qkvg[1:3], preferred_element_type=F32
    )
    keep_rows = (mask_rows == 1)[None, :, None, None]
    is_value = (jnp.arange(2) == 1)[None, None, :, None]
    key_value = jnp.where(keep_rows | is_value, key_value, 0.0).astype(BF)
    key_value = key_value.reshape(samples, 2, tok_rows // 2, 2 * head_width).transpose(1, 0, 2, 3)
    onward = [(i, (i + 1) % row_count) for i in range(row_count)]
    backward = [(i, (i + row_count - 1) % row_count) for i in range(row_count)]
    from_last = lax.ppermute(key_value, "row", onward)
    from_next = lax.ppermute(key_value, "row", backward)
    last_half, next_half = from_last[0], from_next[1]
    far_top = lax.ppermute(last_half, "row", onward)
    far_low = lax.ppermute(next_half, "row", backward)

    pair_tile = pair_rep.transpose(1, 0, 2).astype(F32)
    offsets = jnp.clip(of_rows[0][None, :] - of_cols[0][:, None], -32, 32) + 32
    bin_ids = jnp.where(of_rows[1][None, :] == of_cols[1][:, None], offsets, 65)
    onehot = (
        bin_ids[:, :, None] == jnp.arange(relpos_table.shape[0], dtype=jnp.int32)[None, None, :]
    ).astype(BF)
    pair_in = pair_tile + jnp.einsum(
        "jib,bc->jic", onehot, relpos_table, preferred_element_type=F32
    )
    normed = normalize(pair_in, 2).astype(BF)
    projected = jnp.einsum(
        "jic,ce->eji", normed, proj_in[:, : 4 * channels], preferred_element_type=F32
    )
    pair_mask = (mask_cols[:, None] * mask_rows[None, :]).astype(F32)[None]
    left_in = (
        jax.nn.sigmoid(projected[2 * channels : 3 * channels]) * projected[:channels] * pair_mask
    ).astype(BF)
    right_in = (
        jax.nn.sigmoid(projected[3 * channels :]) * projected[channels : 2 * channels] * pair_mask
    ).astype(BF)
    everywhere = ("row", "col", "near")
    count = row_count * col_count * near_count
    send = jnp.stack([left_in, right_in], axis=1).reshape(count, 2 * col_width, tok_rows)
    got = lax.all_to_all(send, everywhere, 0, 0, tiled=True)
    got = got.reshape(row_count, col_count, near_count, 2, col_width, tok_rows)
    left_own, right_own = got[:, :, :, 0], got[:, :, :, 1]
    left_other = lax.ppermute(left_own, "core", SWAP)
    first = core_at == 0
    left_all = (
        jnp.stack(
            [jnp.where(first, left_own, left_other), jnp.where(first, left_other, left_own)],
            axis=3,
        )
        .transpose(0, 2, 3, 1, 4, 5)
        .reshape(row_count, grp_count, tok_rows, tok_rows)
    )
    right_all = right_own.reshape(row_count, col_count * near_count * col_width, tok_rows)
    triangle = jnp.einsum("rgik,rjk->gji", left_all, right_all, preferred_element_type=F32)
    back = triangle.astype(BF).reshape(count, col_width, tok_rows)
    tri_local = lax.all_to_all(back, everywhere, 0, 0, tiled=True)
    tri_local = tri_local.reshape(channels, col_width, tok_rows)
    out_normed = normalize(tri_local.astype(F32), 0).astype(BF)
    bias_scaled = lax.optimization_barrier(bias_weight * LOG2E)
    key_tile = lax.optimization_barrier(
        jnp.broadcast_to((mask_cols == 1).astype(F32)[:, None], (col_width, tok_rows))
    )
    gate_out = jax.nn.sigmoid(
        jnp.einsum("jic,cd->jid", normed, proj_in[:, 4 * channels :], preferred_element_type=F32)
    )
    update = jnp.einsum("cji,cd->jid", out_normed, out_proj, preferred_element_type=F32)
    pair_new = pair_in + gate_out * update
    pair_out = pair_new.astype(BF).transpose(1, 0, 2)
    bias_local = jnp.einsum(
        "jic,ch->hji", normalize(pair_new, 2), bias_scaled, precision=lax.Precision.HIGHEST
    )
    bias_local = jnp.where(key_tile[None] > 0.5, bias_local, HIDDEN).astype(jnp.float16)
    copies = jnp.broadcast_to(
        bias_local.reshape(grp_count, 1, heads, col_width, tok_rows),
        (grp_count, col_count, heads, col_width, tok_rows),
    ).reshape(grp_count * col_count, heads, col_width, tok_rows)
    bias_all = lax.all_to_all(copies, ("near", "core", "col"), 0, 0, tiled=True)
    bias_all = bias_all.astype(F32)
    bias_all = jnp.where(bias_all > 0.5 * HIDDEN, bias_all, -1000000000.0 * LOG2E)

    query_t = jnp.einsum("srd,de->ser", normed_x, w_qkvg[0], preferred_element_type=F32).astype(BF)
    gate_t = jax.nn.sigmoid(
        jnp.einsum("srd,de->ser", normed_x, w_qkvg[3], preferred_element_type=F32)
    )
    back_t = jnp.einsum("srd,ed->ser", cotangent, w_out, preferred_element_type=F32)
    d_mixed_t = (back_t * gate_t).astype(BF)
    w_far = lax.ppermute(w_out, "near", SWAP)
    w_near = lax.ppermute(w_out, "core", SWAP)
    w_both = lax.ppermute(w_far, "core", SWAP)
    weights = jnp.concatenate([w_out, w_far, w_near, w_both], axis=0)
    keys = row_count * tok_rows
    vmem = pl.BlockSpec(memory_space=pltpu.VMEM)
    by_sample = pl.BlockSpec((1, head_width, tok_rows), lambda s: (s, 0, 0))
    of_tokens = pl.BlockSpec((2, 1, tok_rows // 2, 2 * head_width), lambda s: (0, s, 0, 0))
    gated_t, grads = pl.pallas_call(
        lambda *refs: attention_kernel(heads, head_size, *refs),
        out_shape=(
            pltpu.VMEM((samples, head_width, tok_rows), BF),
            pltpu.VMEM((col_count, heads, keys // col_count, tok_rows), BF),
        ),
        compiler_params=pltpu.CompilerParams(
            vmem_limit_bytes=24 << 20, dimension_semantics=("arbitrary",)
        ),
        grid=(samples,),
        in_specs=[pl.BlockSpec(memory_space=pltpu.SMEM)]
        + [by_sample] * 3
        + [of_tokens] * 3
        + [vmem] * 3,
        out_specs=(by_sample, vmem),
        scratch_shapes=[
            pltpu.VMEM((keys, head_width), BF),
            pltpu.VMEM((keys, head_width), BF),
            pltpu.VMEM((head_width, heads * tok_rows), BF),
            pltpu.VMEM((head_width, heads * tok_rows), BF),
            pltpu.VMEM((keys, heads * tok_rows), F32),
            pltpu.VMEM((keys, heads * tok_rows), F32),
            pltpu.VMEM((keys, heads * tok_rows), BF),
            pltpu.VMEM((keys, heads * tok_rows), F32),
        ],
        name="attention",
    )(
        row_at.astype(jnp.int32).reshape(1),
        *[
            pltpu.with_memory_space_constraint(value, pltpu.HBM)
            for value in (
                query_t,
                d_mixed_t,
                gate_t,
                key_value,
                from_last,
                from_next,
            )
        ],
        pltpu.with_memory_space_constraint(far_top, pltpu.VMEM),
        pltpu.with_memory_space_constraint(far_low, pltpu.VMEM),
        pltpu.with_memory_space_constraint(bias_all, pltpu.VMEM),
    )
    gated_parts = gather_grp(gated_t, 1)
    grad_parts = lax.all_to_all(grads, "col", 0, 0, tiled=True)
    grad_sum = jnp.sum(grad_parts.astype(F32), axis=0)
    bias_grad = grad_sum.transpose(0, 2, 1)
    mixed_out = jnp.einsum(
        "ser,ed->srd",
        gated_parts,
        weights,
        preferred_element_type=F32,
    )
    single_out = (single_rep.astype(F32) + mixed_out).astype(BF)
    return (pair_out, single_out, bias_grad)


def solution(mesh):
    grp, row, col = (mesh.shape[name] for name in ("grp", "row", "col"))
    split = Mesh(mesh.devices.reshape(grp // 2, 2, row, col), ("near", "core", "row", "col"))
    both = ("near", "core")
    placed = (
        P("row", (*both, "col"), None),
        P(),
        P(),
        P(),
        P(),
        P(),
        P(),
        P(),
        P("col", "row", None),
        P(None, None, both),
        P(both, None),
        P("col", "row", None),
    )

    return jax.shard_map(
        on_device,
        mesh=split,
        in_specs=placed,
        out_specs=(P("row", (*both, "col"), None), P("col", "row", None), P(both, "row", "col")),
        check_vma=False,
    )
```
